256 devices in a mesh: row: 64 (over x, z, core), col: 4 (over y).
Axes of the slice: x: 4, y: 4, z: 8, core: 2. Of those that a mesh axis runs over, the one named last changes fastest.
Arguments:
- input_picture: bfloat16 [1024, 512, 256], P('row', 'col'), may hold values from -6 to 6
- spatial_taps_first: bfloat16 [2, 49, 256], replicated, may hold values from -0.875 to 0.875
- widening_matrix_first: bfloat16 [2, 256, 1024], replicated, may hold values from -0.375 to 0.375
- narrowing_matrix_first: bfloat16 [2, 1024, 256], replicated, may hold values from -0.1875 to 0.1875
- stride_kernel_matrix: bfloat16 [1024, 512], replicated, may hold values from -0.1875 to 0.1875
- spatial_taps_second: bfloat16 [2, 49, 512], replicated, may hold values from -0.875 to 0.875
- widening_matrix_second: bfloat16 [2, 512, 2048], replicated, may hold values from -0.25 to 0.25
- narrowing_matrix_second: bfloat16 [2, 2048, 512], replicated, may hold values from -0.125 to 0.125
- sky_clarity_marks: int32 [8, 4], replicated, may hold values 0 or 1
Outputs:
- features: bfloat16 [512, 256, 512], P('row', 'col')
The draws below stay inside these ranges and needn't reach their ends.
Inputs may be any that keep to these rules, and one draw needn't show every extreme that they name: `sky_clarity_marks`: 1 marks a tile of 64 x 64 section-two pixels whose blocks are applied, 0 a cloudy tile that passes through section two unchanged.
All inputs are finite; a program needn't handle non-finite values.
Results may differ from the reference program's by a relative error of at most 0.022.
Values may be sent and summed in bfloat16 or wider, within the bound.
No kernel may reach another device: no remote copies, remote signals or barrier semaphores. Data moves between devices by JAX's collectives and lax.ppermute only.
A program may use at most 128 MiB of HBM per device.

```python
import jax
import jax.numpy as jnp
from jax import lax

FIRST_DEPTH = 256
SECOND_DEPTH = 512
HID1 = 1024
HID2 = 2048
NB1 = 2
NB2 = 2
TILE2 = 64
R_DEV = 16
H = 1024
W = 512
H2 = 512
W2 = 256


def touch_ends(array, key, least, high):
    longest = array.shape.index(max(array.shape))
    spots = []
    for shift in (0, 1):
        where = [jax.random.randint(jax.random.fold_in(key, axis), (), 0, length) for axis, length in enumerate(array.shape)]
        where[longest] = (where[longest] + shift) % array.shape[longest]
        spots.append(tuple(where))
    return array.at[spots[0]].set(least).at[spots[1]].set(high)


def block_scale(own_key, dims, pieces, smallest, top_value):
    def one(dim, parts):
        heights = jax.random.uniform(jax.random.fold_in(jax.random.fold_in(own_key, 6), dim), (parts,), jnp.float32, smallest / len(pieces), top_value / len(pieces))
        return jnp.repeat(jnp.exp(heights), dims[dim] // parts).reshape((-1,) + (1,) * (len(dims) - dim - 1))

    level = one(*pieces[0])
    for cut in pieces[1:]:
        level = level * one(*cut)
    return level


def noise(own_key, shape, width, reach, cuts=(), kind=jnp.bfloat16):
    array = width * jax.random.normal(own_key, shape, jnp.float32)
    if cuts:
        array = array * block_scale(own_key, shape, cuts, -0.22, 0.18)
    return jnp.clip(array, -reach, reach).astype(kind)


def setup_inputs(seed: int = 0) -> dict:
    keys = jax.random.split(jax.random.key(seed), 10)
    return {
        "input_picture": noise(keys[0], (H, W, FIRST_DEPTH), 1.0, 6.0, ((0, 64), (1, 4))),
        "spatial_taps_first": noise(keys[1], (NB1, 49, FIRST_DEPTH), 49 ** -0.5, 0.875),
        "widening_matrix_first": noise(keys[2], (NB1, FIRST_DEPTH, HID1), FIRST_DEPTH ** -0.5, 0.375),
        "narrowing_matrix_first": noise(keys[3], (NB1, HID1, FIRST_DEPTH), HID1 ** -0.5, 0.1875),
        "stride_kernel_matrix": noise(keys[4], (4 * FIRST_DEPTH, SECOND_DEPTH), (4 * FIRST_DEPTH) ** -0.5, 0.1875),
        "spatial_taps_second": noise(keys[5], (NB2, 49, SECOND_DEPTH), 49 ** -0.5, 0.875),
        "widening_matrix_second": noise(keys[6], (NB2, SECOND_DEPTH, HID2), SECOND_DEPTH ** -0.5, 0.25),
        "narrowing_matrix_second": noise(keys[7], (NB2, HID2, SECOND_DEPTH), HID2 ** -0.5, 0.125),
        "sky_clarity_marks": touch_ends((jax.random.randint(keys[8], (H2 // TILE2, W2 // TILE2), 0, 2) < 1).astype(jnp.int32), jax.random.fold_in(keys[8], 1), 0, 1),
    }


epsilon = 1e-06

def depthwise(padded, kernel_taps, vertical_extent, lateral_extent):
    weights = kernel_taps.astype(jnp.float32)
    accumulated = jnp.zeros((vertical_extent, lateral_extent, padded.shape[-1]), jnp.float32)
    for tap_row in range(7):
        for tap_col in range(7):
            window = padded[tap_row:tap_row + vertical_extent, tap_col:tap_col + lateral_extent, :].astype(jnp.float32)
            accumulated = accumulated + window * weights[7 * tap_row + tap_col]
    return accumulated

def normalize(values):
    mean_pooled = lax.optimization_barrier(jnp.mean(values, axis=-1, keepdims=True))
    centred = values - mean_pooled
    variance = lax.optimization_barrier(jnp.mean(centred * centred, axis=-1, keepdims=True))
    return centred / jnp.sqrt(variance + epsilon)

def expand(flattened, w_in, w_out):
    hidden = jax.nn.gelu(jnp.dot(flattened, w_in, preferred_element_type=jnp.float32), approximate=False).astype(jnp.bfloat16)
    return jnp.dot(hidden, w_out, preferred_element_type=jnp.float32)

def block_branch(padded, kernel_taps, w_in, w_out, vertical_extent, lateral_extent):
    channels = padded.shape[-1]
    mixture = depthwise(padded, kernel_taps, vertical_extent, lateral_extent)
    flattened = normalize(mixture).astype(jnp.bfloat16).reshape(vertical_extent * lateral_extent, channels)
    return expand(flattened, w_in, w_out).reshape(vertical_extent, lateral_extent, channels)

def whole_branch(activation_tensor, kernel_taps, w_in, w_out, band_rows):
    vertical_extent, lateral_extent, channels = activation_tensor.shape
    padded = jnp.pad(activation_tensor, ((3, 3), (3, 3), (0, 0)))

    def one_band(band_index):
        first_row = (band_index * band_rows).astype(jnp.int32)
        portion = lax.dynamic_slice_in_dim(padded, first_row, band_rows + 6, 0)
        return block_branch(portion, kernel_taps, w_in, w_out, band_rows, lateral_extent)
    bands = lax.map(one_band, jnp.arange(vertical_extent // band_rows, dtype=jnp.int32))
    return bands.reshape(vertical_extent, lateral_extent, channels)

def halve_spacing(activation_tensor, stride_kernel_matrix):
    vertical_extent, lateral_extent, channels = activation_tensor.shape
    normed = normalize(activation_tensor.astype(jnp.float32)).astype(jnp.bfloat16)
    patch_blocks = normed.reshape(vertical_extent // 2, 2, lateral_extent // 2, 2, channels).transpose(0, 2, 1, 3, 4)
    patch_blocks = patch_blocks.reshape(vertical_extent // 2 * (lateral_extent // 2), 4 * channels)
    final_answer = jnp.dot(patch_blocks, stride_kernel_matrix, preferred_element_type=jnp.float32).astype(jnp.bfloat16)
    return final_answer.reshape(vertical_extent // 2, lateral_extent // 2, stride_kernel_matrix.shape[1])

def reference(input_picture, spatial_taps_first, widening_matrix_first, narrowing_matrix_first, stride_kernel_matrix, spatial_taps_second, widening_matrix_second, narrowing_matrix_second, sky_clarity_marks):
    running_activation = input_picture
    for layer_index in range(NB1):
        branch = whole_branch(running_activation, spatial_taps_first[layer_index], widening_matrix_first[layer_index], narrowing_matrix_first[layer_index], R_DEV)
        running_activation = (running_activation.astype(jnp.float32) + branch).astype(jnp.bfloat16)
    halved_lattice = halve_spacing(running_activation, stride_kernel_matrix)
    keep = jnp.repeat(jnp.repeat(sky_clarity_marks, TILE2, axis=0), TILE2, axis=1) == 1
    for layer_index in range(NB2):
        branch = whole_branch(halved_lattice, spatial_taps_second[layer_index], widening_matrix_second[layer_index], narrowing_matrix_second[layer_index], R_DEV // 2)
        updated = (halved_lattice.astype(jnp.float32) + branch).astype(jnp.bfloat16)
        halved_lattice = jnp.where(keep[:, :, None], updated, halved_lattice)
    return halved_lattice
```

```python
import functools

import jax
import jax.numpy as jnp
import numpy as np
from jax import lax
from jax.experimental import pallas as pl
from jax.experimental.pallas import tpu as pltpu
from jax.sharding import PartitionSpec as P

TILE2 = 64
EPS = 1e-06
F32 = jnp.float32
BF16 = jnp.bfloat16
S = 16
PAD = 8
RING = 6


def spread(width):
    planes = width // S
    hot = np.zeros((planes + 6, S, width), np.float32)
    for t in range(-3, planes + 3):
        for s in range(S):
            c = planes * s + t
            if 0 <= c < width:
                hot[t + 3, s, c] = 1
    return hot.reshape((planes + 6) * S, width)


def pick(width, columns):
    planes = width // S
    hot = np.zeros((len(columns), width), np.float32)
    for j, c in enumerate(columns):
        s, t = divmod(c + PAD, planes)
        hot[j, t * S + s] = 1
    return hot


def dot(a, b):
    return jnp.dot(a, b, preferred_element_type=F32)


def spread_taps(taps_ref, layer, wide_ref):
    taps = taps_ref[layer].astype(F32)
    for tap in range(49):
        row = jnp.broadcast_to(taps[tap : tap + 1], (S, taps.shape[1]))
        wide_ref[tap] = row.astype(BF16)


def depthwise(field_ref, row, wide_ref, planes, lanes):
    total = None
    for a in range(7):
        line = field_ref[row + a, :, :, lanes]
        p = [line[b : b + planes] * wide_ref[7 * a + b, :, lanes][None] for b in range(7)]
        part = ((p[0] + p[1]) + (p[2] + p[3])) + ((p[4] + p[5]) + p[6])
        part = part.astype(F32)
        total = part if total is None else total + part
    return total


def normalize(parts):
    depth = 128 * len(parts)
    mean = jnp.sum(functools.reduce(jnp.add, parts), axis=-1, keepdims=True) / depth
    centred = [p - mean for p in parts]
    squares = functools.reduce(jnp.add, [c * c for c in centred])
    variance = jnp.sum(squares, axis=-1, keepdims=True) / depth
    scale = lax.rsqrt(variance + EPS)
    return jnp.concatenate([c * scale for c in centred], axis=-1).astype(BF16)


def gelu(h):
    return (0.5 * h * (1.0 + lax.erf(h * np.float32(0.5**0.5)))).astype(BF16)


def mlp(flat, w_in_ref, w_out_ref, layer, step):
    hidden = w_in_ref.shape[2]
    total = None
    for c in range(0, hidden, step):
        h = gelu(dot(flat, w_in_ref[layer, :, c : c + step]))
        part = dot(h, w_out_ref[layer, c : c + step, :])
        total = part if total is None else total + part
    return total


def store_planes(field_ref, row, values, planes):
    field_ref[row, 3 : 3 + planes] = values.astype(BF16)
    for j in range(3):
        field_ref[row, j] = pltpu.roll(values[planes - 3 + j], 1, 0).astype(BF16)
        field_ref[row, 3 + planes + j] = pltpu.roll(values[j], S - 1, 0).astype(BF16)


def column_index(planes):
    t = lax.broadcasted_iota(jnp.int32, (planes, S, 1), 0)
    s = lax.broadcasted_iota(jnp.int32, (planes, S, 1), 1)
    return planes * s + t - PAD


def section_one(
    bounds_ref, x_ref, spread_ref, pick_ref, taps_ref, w_in_ref, w_out_ref, stride_ref,
    out_ref, field0, field1, wide, patches,
):
    rows = x_ref.shape[0] - 2 * RING
    width, depth = x_ref.shape[1:]
    planes = width // S
    pixels = planes * S
    halves = [pl.ds(128 * c, 128) for c in range(depth // 128)]
    columns = column_index(planes)
    inside = (columns >= bounds_ref[2]) & (columns < bounds_ref[3])

    def permute(r, carry):
        field0[r] = dot(spread_ref[...], x_ref[r]).astype(BF16).reshape(planes + 6, S, depth)
        return carry

    lax.fori_loop(0, rows + 2 * RING, permute, 0)

    def block(field_ref, layer, row):
        parts = [
            jnp.concatenate([depthwise(field_ref, row + i, wide, planes, h) for i in range(2)], 0)
            for h in halves
        ]
        flat = normalize(parts).reshape(2 * pixels, depth)
        branch = mlp(flat, w_in_ref, w_out_ref, layer, 256).reshape(2, planes, S, depth)
        return [field_ref[row + i + 3, 3 : 3 + planes].astype(F32) + branch[i] for i in range(2)]

    spread_taps(taps_ref, 0, wide)

    def first(g, carry):
        values = block(field0, 0, 2 * g)
        for i in range(2):
            r = 2 * g + i - 3
            keep = inside & (r >= bounds_ref[0]) & (r < bounds_ref[1])
            store_planes(field1, 2 * g + i, jnp.where(keep, values[i], 0.0), planes)
        return carry

    lax.fori_loop(0, (rows + 6) // 2, first, 0)
    spread_taps(taps_ref, 1, wide)

    def second(g, carry):
        values = block(field1, 1, 2 * g)
        for dy in range(2):
            rounded = values[dy].astype(BF16).astype(F32)
            normed = normalize([rounded[:, :, 128 * c : 128 * c + 128] for c in range(depth // 128)])
            chosen = dot(pick_ref[...], normed.reshape(pixels, depth)).astype(BF16)
            half = chosen.shape[0] // 2
            for dx in range(2):
                at = (2 * dy + dx) * depth
                patches[g, :, at : at + depth] = chosen[dx * half : (dx + 1) * half]
        return carry

    lax.fori_loop(0, rows // 2, second, 0)
    coarse = dot(patches[...].reshape(-1, 4 * depth), stride_ref[...])
    out_ref[...] = coarse.astype(BF16).reshape(out_ref.shape)


def section_two(
    bounds_ref, flags_ref, z_ref, spread_ref, pick_ref, taps_ref, w_in_ref, w_out_ref,
    out_ref, field0, field1, wide, flats, total,
):
    rows, cols = out_ref.shape[:2]
    width, depth = z_ref.shape[1:]
    hidden = w_in_ref.shape[2]
    planes = width // S
    pixels = planes * S
    groups = [pl.ds(128 * c, 128) for c in range(depth // 128)]
    step = 512

    @pl.when(flags_ref[4] == 0)
    def _():
        out_ref[...] = z_ref[RING : RING + rows, PAD : PAD + cols, :]

    @pl.when(flags_ref[4] != 0)
    def _():
        columns = column_index(planes)
        inside = (columns >= bounds_ref[2]) & (columns < bounds_ref[3])

        def permute(r, carry):
            field0[r] = dot(spread_ref[...], z_ref[r]).astype(BF16).reshape(planes + 6, S, depth)
            return carry

        lax.fori_loop(0, rows + 2 * RING, permute, 0)

        def block(field_ref, layer, count):
            spread_taps(taps_ref, layer, wide)

            def one(r, carry):
                parts = [depthwise(field_ref, r, wide, planes, c) for c in groups]
                flats[r] = normalize(parts).reshape(pixels, depth)
                return carry

            lax.fori_loop(0, count, one, 0)
            half = count // 2
            for q in range(2):
                flat = flats[q * half : (q + 1) * half].reshape(half * pixels, depth)
                branch = mlp(flat, w_in_ref, w_out_ref, layer, step)
                total[q * half : (q + 1) * half] = branch.reshape(half, planes, S, depth)

        block(field0, 0, rows + 6)

        def merge(band):
            def one(r, carry):
                old = field0[r + 3, 3 : 3 + planes].astype(F32)
                left, mid, right = [flags_ref[3 * band + k] for k in range(3)]
                flag = jnp.where(columns < 0, left, jnp.where(columns < cols, mid, right))
                new = jnp.where(flag != 0, old + total[r], old)
                own = r - 3
                keep = inside & (own >= bounds_ref[0]) & (own < bounds_ref[1])
                store_planes(field1, r, jnp.where(keep, new, 0.0), planes)
                return carry

            return one

        lax.fori_loop(0, 3, merge(0), 0)
        lax.fori_loop(3, rows + 3, merge(1), 0)
        lax.fori_loop(rows + 3, rows + 6, merge(2), 0)
        block(field1, 1, rows)

        def finish(r, carry):
            new = field1[r + 3, 3 : 3 + planes].astype(F32) + total[r]
            new = new.astype(BF16).reshape(pixels, depth)
            out_ref[r] = dot(pick_ref[...], new).astype(BF16)
            return carry

        lax.fori_loop(0, rows, finish, 0)


def with_halo(cells):
    for axis, dim, width in (("col", 1, PAD), ("row", 0, RING)):
        ends = lax.axis_size(axis) - 1
        head = lax.slice_in_dim(cells, 0, width, axis=dim)
        tail = lax.slice_in_dim(cells, cells.shape[dim] - width, cells.shape[dim], axis=dim)
        before = lax.ppermute(tail, axis, [(i, i + 1) for i in range(ends)])
        after = lax.ppermute(head, axis, [(i + 1, i) for i in range(ends)])
        cells = jnp.concatenate([before, cells, after], axis=dim)
    return cells


def call(kernel, name, out_shape, scalars, arrays, scratch):
    return pl.pallas_call(
        kernel,
        name=name,
        out_shape=out_shape,
        in_specs=[pl.BlockSpec(memory_space=pltpu.SMEM) for _ in scalars]
        + [pl.BlockSpec(memory_space=pltpu.VMEM) for _ in arrays],
        out_specs=pl.BlockSpec(memory_space=pltpu.VMEM),
        scratch_shapes=[pltpu.VMEM(shape, dtype) for shape, dtype in scratch],
        compiler_params=pltpu.CompilerParams(vmem_limit_bytes=56 * 1024 * 1024),
    )(*scalars, *arrays)


def run_one(bounds, padded, taps, w_in, w_out, stride):
    rows, width, depth = padded.shape
    rows -= 2 * RING
    planes = width // S
    half = (width - 2 * PAD) // 2
    wide_depth = stride.shape[1]
    columns = [2 * j + dx for dx in range(2) for j in range(half)]
    return call(
        section_one,
        "section_one",
        jax.ShapeDtypeStruct((rows // 2, half, wide_depth), BF16),
        [bounds],
        [padded, jnp.asarray(spread(width), BF16), jnp.asarray(pick(width, columns), BF16),
         taps, w_in, w_out, stride],
        [
            ((rows + 2 * RING, planes + 6, S, depth), BF16),
            ((rows + 6, planes + 6, S, depth), BF16),
            ((49, S, depth), BF16),
            ((rows // 2, half, 4 * depth), BF16),
        ],
    )


def run_two(bounds, flags, padded, taps, w_in, w_out):
    rows, width, depth = padded.shape
    rows -= 2 * RING
    cols = width - 2 * PAD
    planes = width // S
    return call(
        section_two,
        "section_two",
        jax.ShapeDtypeStruct((rows, cols, depth), BF16),
        [bounds, flags],
        [padded, jnp.asarray(spread(width), BF16), jnp.asarray(pick(width, range(cols)), BF16),
         taps, w_in, w_out],
        [
            ((rows + 2 * RING, planes + 6, S, depth), BF16),
            ((rows + 6, planes + 6, S, depth), BF16),
            ((49, S, depth), BF16),
            ((rows + 6, planes * S, depth), BF16),
            ((rows + 6, planes, S, depth), F32),
        ],
    )


def edges(rows, cols):
    i, j = lax.axis_index("row"), lax.axis_index("col")
    last_i, last_j = lax.axis_size("row") - 1, lax.axis_size("col") - 1
    far = 1 << 20
    return jnp.stack([
        jnp.where(i == 0, 0, -far),
        jnp.where(i == last_i, rows, far),
        jnp.where(j == 0, 0, -far),
        jnp.where(j == last_j, cols, far),
    ]).astype(jnp.int32)


def tile_flags(marks, rows, cols):
    i, j = lax.axis_index("row") * rows, lax.axis_index("col") * cols
    down = jnp.stack([i - 1, i, i + rows]) // TILE2
    across = jnp.stack([j - 1, j, j + cols]) // TILE2
    down = jnp.clip(down, 0, marks.shape[0] - 1)
    across = jnp.clip(across, 0, marks.shape[1] - 1)
    return (marks[down][:, across] == 1).astype(jnp.int32).reshape(9)


def per_device(
    input_picture,
    spatial_taps_first,
    widening_matrix_first,
    narrowing_matrix_first,
    stride_kernel_matrix,
    spatial_taps_second,
    widening_matrix_second,
    narrowing_matrix_second,
    sky_clarity_marks,
):
    rows, cols = input_picture.shape[:2]
    coarse = run_one(
        edges(rows, cols),
        with_halo(input_picture),
        spatial_taps_first,
        widening_matrix_first,
        narrowing_matrix_first,
        stride_kernel_matrix,
    )
    return run_two(
        edges(rows // 2, cols // 2),
        tile_flags(sky_clarity_marks, rows // 2, cols // 2),
        with_halo(coarse),
        spatial_taps_second,
        widening_matrix_second,
        narrowing_matrix_second,
    )


def solution(mesh):
    placed = (P("row", "col", None), P(), P(), P(), P(), P(), P(), P(), P())
    return jax.shard_map(
        per_device, mesh=mesh, in_specs=placed, out_specs=P("row", "col", None), check_vma=False
    )
```

```python
import functools

import jax
import jax.numpy as jnp
import numpy as np
from jax import lax
from jax.experimental import pallas as pl
from jax.experimental.pallas import tpu as pltpu
from jax.sharding import PartitionSpec as P

TILE2 = 64
EPS = 1e-06
F32 = jnp.float32
BF16 = jnp.bfloat16
S = 16
PAD = 8
RING = 6
GROUP = 2


def spread(width):
    planes = width // S
    hot = np.zeros((planes + 6, S, width), np.float32)
    for t in range(-3, planes + 3):
        for s in range(S):
            c = planes * s + t
            if 0 <= c < width:
                hot[t + 3, s, c] = 1
    return hot.reshape((planes + 6) * S, width)


def pick(width, columns):
    planes = width // S
    hot = np.zeros((len(columns), width), np.float32)
    for j, c in enumerate(columns):
        s, t = divmod(c + PAD, planes)
        hot[j, t * S + s] = 1
    return hot


def dot(a, b):
    return jnp.dot(a, b, preferred_element_type=F32)


def spread_taps(taps_ref, layer, wide_ref):
    taps = taps_ref[layer].astype(F32)
    for tap in range(49):
        wide_ref[tap] = jnp.broadcast_to(taps[tap : tap + 1], wide_ref.shape[1:])


def depthwise(field_ref, row, wide_ref, planes, lanes):
    total = [None] * planes
    for a in range(7):
        line = field_ref[row + a, :, :, lanes].astype(F32).reshape(planes + 6, S // 8, 8, 128)
        for b in range(7):
            tap = wide_ref[7 * a + b, :, lanes][None]
            for t in range(planes):
                p = line[t + b] * tap
                total[t] = p if total[t] is None else total[t] + p
    return jnp.stack(total).reshape(planes, S, 128)


def normalize(parts):
    depth = 128 * len(parts)
    mean = jnp.sum(functools.reduce(jnp.add, parts), axis=-1, keepdims=True) / depth
    centred = [p - mean for p in parts]
    squares = functools.reduce(jnp.add, [c * c for c in centred])
    variance = jnp.sum(squares, axis=-1, keepdims=True) / depth
    scale = lax.rsqrt(variance + EPS)
    return jnp.concatenate([c * scale for c in centred], axis=-1).astype(BF16)


def twice_gelu(h):
    return (h * (1.0 + lax.erf(h * np.float32(0.5**0.5)))).astype(BF16)


def mlp(flat, w_in_ref, w_out_ref, layer, step):
    hidden = w_in_ref.shape[2]
    total = None
    for c in range(0, hidden, step):
        h = twice_gelu(dot(flat, w_in_ref[layer, :, c : c + step]))
        part = dot(h, w_out_ref[layer, c : c + step, :])
        total = part if total is None else total + part
    return 0.5 * total


def run_block(
    field_ref, count, group, layer, taps_ref, w_in_ref, w_out_ref, wide, mixed, step, ahead, emit
):
    planes, depth = field_ref.shape[1] - 6, field_ref.shape[3]
    chunks = depth // 128
    spread_taps(taps_ref, layer, wide)

    def mix(g):
        for i in range(group):
            for c in range(chunks):
                sums = depthwise(field_ref, group * g + i, wide, planes, pl.ds(128 * c, 128))
                mixed[g % 2, c, i] = sums

    def project(g):
        flat = normalize([mixed[g % 2, c] for c in range(chunks)])
        flat = flat.reshape(group * planes * S, depth)
        branch = mlp(flat, w_in_ref, w_out_ref, layer, step)
        emit(g, branch.reshape(group, planes, S, depth))

    mix(0)

    def body(g, carry):
        if ahead:
            mix(g + 1)
        project(g)
        if not ahead:
            mix(g + 1)
        return carry

    last = count // group - 1
    lax.fori_loop(0, last, body, 0)
    project(last)


def store_planes(field_ref, row, values, planes):
    field_ref[row, 3 : 3 + planes] = values.astype(BF16)
    for j in range(3):
        field_ref[row, j] = pltpu.roll(values[planes - 3 + j], 1, 0).astype(BF16)
        field_ref[row, 3 + planes + j] = pltpu.roll(values[j], S - 1, 0).astype(BF16)


def column_index(planes):
    t = lax.broadcasted_iota(jnp.int32, (planes, S, 1), 0)
    s = lax.broadcasted_iota(jnp.int32, (planes, S, 1), 1)
    return planes * s + t - PAD


def permute_rows(spread_ref, source_ref, field_ref, unroll):
    shape = field_ref.shape[1:]

    def one(r, carry):
        field_ref[r] = dot(spread_ref[...], source_ref[r]).astype(BF16).reshape(shape)
        return carry

    lax.fori_loop(0, source_ref.shape[0], one, 0, unroll=unroll)


def picture_edges(place_ref, ends, columns, rows, cols):
    far = 1 << 20
    top = jnp.where(place_ref[0] == 0, 0, -far)
    bottom = jnp.where(place_ref[0] == ends[0], rows, far)
    left = jnp.where(place_ref[1] == 0, 0, -far)
    right = jnp.where(place_ref[1] == ends[1], cols, far)
    return top, bottom, (columns >= left) & (columns < right)


def section_one(
    ends, place_ref, x_ref, spread_ref, pick_ref, taps_ref, w_in_ref, w_out_ref, stride_ref,
    out_ref, field0, field1, wide, mixed, patches,
):
    rows = x_ref.shape[0] - 2 * RING
    width, depth = x_ref.shape[1:]
    planes = width // S
    pixels = planes * S
    columns = column_index(planes)
    top, bottom, inside = picture_edges(place_ref, ends, columns, rows, width - 2 * PAD)
    permute_rows(spread_ref, x_ref, field0, 4)

    def first(g, branch):
        for i in range(GROUP):
            at = GROUP * g + i
            value = field0[at + 3, 3 : 3 + planes].astype(F32) + branch[i]
            keep = inside & (at - 3 >= top) & (at - 3 < bottom)
            store_planes(field1, at, jnp.where(keep, value, 0.0), planes)

    def second(g, branch):
        for dy in range(2):
            value = field1[2 * g + dy + 3, 3 : 3 + planes].astype(F32) + branch[dy]
            value = value.astype(BF16).astype(F32)
            normed = normalize([value[:, :, 128 * c : 128 * c + 128] for c in range(depth // 128)])
            chosen = dot(pick_ref[...], normed.reshape(pixels, depth)).astype(BF16)
            half = chosen.shape[0] // 2
            for dx in range(2):
                at = (2 * dy + dx) * depth
                patches[g, :, at : at + depth] = chosen[dx * half : (dx + 1) * half]

    weights = (taps_ref, w_in_ref, w_out_ref, wide, mixed, 256, False)
    run_block(field0, rows + 6, GROUP, 0, *weights, first)
    run_block(field1, rows, 2, 1, *weights, second)
    coarse = dot(patches[...].reshape(-1, 4 * depth), stride_ref[...])
    out_ref[...] = coarse.astype(BF16).reshape(out_ref.shape)


def section_two(
    ends, place_ref, marks_ref, z_ref, spread_ref, pick_ref, taps_ref, w_in_ref, w_out_ref,
    out_ref, field0, field1, wide, mixed,
):
    rows, cols = out_ref.shape[:2]
    width, depth = z_ref.shape[1:]
    planes = width // S
    pixels = planes * S

    def tile_flag(i, j):
        i = jnp.clip((place_ref[0] * rows + i) // TILE2, 0, marks_ref.shape[0] - 1)
        j = jnp.clip((place_ref[1] * cols + j) // TILE2, 0, marks_ref.shape[1] - 1)
        return marks_ref[i, j]

    clear = tile_flag(0, 0) == 1

    @pl.when(jnp.logical_not(clear))
    def _():
        out_ref[...] = z_ref[RING : RING + rows, PAD : PAD + cols, :]

    @pl.when(clear)
    def _():
        columns = column_index(planes)
        top, bottom, inside = picture_edges(place_ref, ends, columns, rows, cols)
        permute_rows(spread_ref, z_ref, field0, 4)

        def first(g, branch):
            for i in range(GROUP):
                at = GROUP * g + i
                own = at - 3
                old = field0[at + 3, 3 : 3 + planes].astype(F32)
                left, mid, right = [tile_flag(own, j) for j in (-1, 0, cols)]
                flag = jnp.where(columns < 0, left, jnp.where(columns < cols, mid, right))
                new = jnp.where(flag == 1, old + branch[i], old)
                keep = inside & (own >= top) & (own < bottom)
                store_planes(field1, at, jnp.where(keep, new, 0.0), planes)

        def second(g, branch):
            for i in range(2):
                at = 2 * g + i
                new = field1[at + 3, 3 : 3 + planes].astype(F32) + branch[i]
                new = new.astype(BF16).reshape(pixels, depth)
                out_ref[at] = dot(pick_ref[...], new).astype(BF16)

        weights = (taps_ref, w_in_ref, w_out_ref, wide, mixed, 512, True)
        run_block(field0, rows + 6, GROUP, 0, *weights, first)
        run_block(field1, rows, 2, 1, *weights, second)


def with_halo(cells):
    for axis, dim, width in (("col", 1, PAD), ("row", 0, RING)):
        count = lax.axis_size(axis)
        even = lax.axis_index(axis) % 2 == 0
        head = lax.slice_in_dim(cells, 0, width, axis=dim)
        tail = lax.slice_in_dim(cells, cells.shape[dim] - width, cells.shape[dim], axis=dim)
        inner = [(i, i ^ 1) for i in range(count)]
        outer = [(i, (i - 1 ^ 1) + 1) for i in range(1, count - 1)]
        near = lax.ppermute(jnp.where(even, tail, head), axis, inner)
        far = lax.ppermute(jnp.where(even, head, tail), axis, outer)
        before = jnp.where(even, far, near)
        after = jnp.where(even, near, far)
        cells = jnp.concatenate([before, cells, after], axis=dim)
    return cells


def call(kernel, name, out_shape, scalars, arrays, scratch):
    return pl.pallas_call(
        kernel,
        name=name,
        out_shape=out_shape,
        in_specs=[pl.BlockSpec(memory_space=pltpu.SMEM) for _ in scalars]
        + [pl.BlockSpec(memory_space=pltpu.VMEM) for _ in arrays],
        out_specs=pl.BlockSpec(memory_space=pltpu.VMEM),
        scratch_shapes=[pltpu.VMEM(shape, dtype) for shape, dtype in scratch],
        compiler_params=pltpu.CompilerParams(vmem_limit_bytes=56 * 1024 * 1024),
    )(*scalars, *arrays)


def run_one(ends, place, padded, taps, w_in, w_out, stride):
    rows, width, depth = padded.shape
    rows -= 2 * RING
    planes = width // S
    half = (width - 2 * PAD) // 2
    wide_depth = stride.shape[1]
    columns = [2 * j + dx for dx in range(2) for j in range(half)]
    return call(
        functools.partial(section_one, ends),
        "section_one",
        jax.ShapeDtypeStruct((rows // 2, half, wide_depth), BF16),
        [place],
        [padded, jnp.asarray(spread(width), BF16), jnp.asarray(pick(width, columns), BF16),
         taps, w_in, w_out, stride],
        [
            ((rows + 2 * RING, planes + 6, S, depth), BF16),
            ((rows + 6, planes + 6, S, depth), BF16),
            ((49, 8, depth), F32),
            ((2, depth // 128, GROUP, planes, S, 128), F32),
            ((rows // 2, half, 4 * depth), BF16),
        ],
    )


def run_two(ends, place, marks, padded, taps, w_in, w_out):
    rows, width, depth = padded.shape
    rows -= 2 * RING
    cols = width - 2 * PAD
    planes = width // S
    return call(
        functools.partial(section_two, ends),
        "section_two",
        jax.ShapeDtypeStruct((rows, cols, depth), BF16),
        [place, marks],
        [padded, jnp.asarray(spread(width), BF16), jnp.asarray(pick(width, range(cols)), BF16),
         taps, w_in, w_out],
        [
            ((rows + 2 * RING, planes + 6, S, depth), BF16),
            ((rows + 6, planes + 6, S, depth), BF16),
            ((49, 8, depth), F32),
            ((2, depth // 128, GROUP, planes, S, 128), F32),
        ],
    )


def per_device(
    input_picture,
    spatial_taps_first,
    widening_matrix_first,
    narrowing_matrix_first,
    stride_kernel_matrix,
    spatial_taps_second,
    widening_matrix_second,
    narrowing_matrix_second,
    sky_clarity_marks,
):
    axes = ("row", "col")
    place = jnp.stack([lax.axis_index(axis) for axis in axes]).astype(jnp.int32)
    ends = tuple(lax.axis_size(axis) - 1 for axis in axes)
    coarse = run_one(
        ends,
        place,
        with_halo(input_picture),
        spatial_taps_first,
        widening_matrix_first,
        narrowing_matrix_first,
        stride_kernel_matrix,
    )
    return run_two(
        ends,
        place,
        sky_clarity_marks,
        with_halo(coarse),
        spatial_taps_second,
        widening_matrix_second,
        narrowing_matrix_second,
    )


def solution(mesh):
    placed = (P("row", "col", None), P(), P(), P(), P(), P(), P(), P(), P())
    return jax.shard_map(
        per_device, mesh=mesh, in_specs=placed, out_specs=P("row", "col", None), check_vma=False
    )
```

```python
import functools

import jax
import jax.numpy as jnp
import numpy as np
from jax import lax
from jax.experimental import pallas as pl
from jax.experimental.pallas import tpu as pltpu
from jax.sharding import PartitionSpec as P

TILE2 = 64
EPS = 1e-06
F32 = jnp.float32
BF16 = jnp.bfloat16
S = 16
PAD = 8
RING = 6
GROUP = 2


def spread(width):
    planes = width // S
    hot = np.zeros((planes + 6, S, width), np.float32)
    for t in range(-3, planes + 3):
        for s in range(S):
            c = planes * s + t
            if 0 <= c < width:
                hot[t + 3, s, c] = 1
    return hot.reshape((planes + 6) * S, width)


def pick(width, columns):
    planes = width // S
    hot = np.zeros((len(columns), width), np.float32)
    for j, c in enumerate(columns):
        s, t = divmod(c + PAD, planes)
        hot[j, t * S + s] = 1
    return hot


def dot(a, b):
    return jnp.dot(a, b, preferred_element_type=F32)


def spread_taps(taps_ref, layer, wide_ref):
    taps = taps_ref[layer].astype(F32)
    for tap in range(49):
        wide_ref[tap] = jnp.broadcast_to(taps[tap : tap + 1], wide_ref.shape[1:])


def depthwise(field_ref, row, wide_ref, planes, lanes):
    total = [None] * planes
    for a in range(7):
        line = field_ref[row + a, :, :, lanes].astype(F32).reshape(planes + 6, S // 8, 8, 128)
        for b in range(7):
            tap = wide_ref[7 * a + b, :, lanes][None]
            for t in range(planes):
                p = line[t + b] * tap
                total[t] = p if total[t] is None else total[t] + p
    return jnp.stack(total).reshape(planes, S, 128)


def normalize(parts):
    depth = 128 * len(parts)
    mean = jnp.sum(functools.reduce(jnp.add, parts), axis=-1, keepdims=True) / depth
    centred = [p - mean for p in parts]
    squares = functools.reduce(jnp.add, [c * c for c in centred])
    variance = jnp.sum(squares, axis=-1, keepdims=True) / depth
    scale = lax.rsqrt(variance + EPS)
    return jnp.concatenate([c * scale for c in centred], axis=-1).astype(BF16)


def twice_gelu(h):
    return (h * (1.0 + lax.erf(h * np.float32(0.5**0.5)))).astype(BF16)


def mlp(flat, w_in_ref, w_out_ref, layer, step):
    hidden = w_in_ref.shape[2]
    total = None
    for c in range(0, hidden, step):
        h = twice_gelu(dot(flat, w_in_ref[layer, :, c : c + step]))
        part = dot(h, w_out_ref[layer, c : c + step, :])
        total = part if total is None else total + part
    return 0.5 * total


def run_block(
    field_ref, count, group, layer, taps_ref, w_in_ref, w_out_ref, wide, mixed, step, ahead, emit
):
    planes, depth = field_ref.shape[1] - 6, field_ref.shape[3]
    chunks = depth // 128
    spread_taps(taps_ref, layer, wide)

    def mix(g):
        for i in range(group):
            for c in range(chunks):
                sums = depthwise(field_ref, group * g + i, wide, planes, pl.ds(128 * c, 128))
                mixed[g % 2, c, i] = sums

    def project(g):
        flat = normalize([mixed[g % 2, c] for c in range(chunks)])
        flat = flat.reshape(group * planes * S, depth)
        branch = mlp(flat, w_in_ref, w_out_ref, layer, step)
        emit(g, branch.reshape(group, planes, S, depth))

    mix(0)

    def body(g, carry):
        if ahead:
            mix(g + 1)
        project(g)
        if not ahead:
            mix(g + 1)
        return carry

    last = count // group - 1
    lax.fori_loop(0, last, body, 0)
    project(last)


def store_planes(field_ref, row, values, planes):
    field_ref[row, 3 : 3 + planes] = values.astype(BF16)
    for j in range(3):
        field_ref[row, j] = pltpu.roll(values[planes - 3 + j], 1, 0).astype(BF16)
        field_ref[row, 3 + planes + j] = pltpu.roll(values[j], S - 1, 0).astype(BF16)


def column_index(planes):
    t = lax.broadcasted_iota(jnp.int32, (planes, S, 1), 0)
    s = lax.broadcasted_iota(jnp.int32, (planes, S, 1), 1)
    return planes * s + t - PAD


def permute_rows(spread_ref, source_ref, field_ref, unroll):
    shape = field_ref.shape[1:]

    def one(r, carry):
        field_ref[r] = dot(spread_ref[...], source_ref[r]).astype(BF16).reshape(shape)
        return carry

    lax.fori_loop(0, source_ref.shape[0], one, 0, unroll=unroll)


def picture_edges(place_ref, ends, columns, rows, cols):
    far = 1 << 20
    top = jnp.where(place_ref[0] == 0, 0, -far)
    bottom = jnp.where(place_ref[0] == ends[0], rows, far)
    left = jnp.where(place_ref[1] == 0, 0, -far)
    right = jnp.where(place_ref[1] == ends[1], cols, far)
    return top, bottom, (columns >= left) & (columns < right)


def section_one(
    ends, place_ref, x_ref, spread_ref, pick_ref, taps_ref, w_in_ref, w_out_ref, stride_ref,
    out_ref, field0, field1, wide, mixed, patches,
):
    rows = x_ref.shape[0] - 2 * RING
    width, depth = x_ref.shape[1:]
    planes = width // S
    pixels = planes * S
    columns = column_index(planes)
    top, bottom, inside = picture_edges(place_ref, ends, columns, rows, width - 2 * PAD)
    permute_rows(spread_ref, x_ref, field0, 4)

    def first(g, branch):
        for i in range(GROUP):
            at = GROUP * g + i
            value = field0[at + 3, 3 : 3 + planes].astype(F32) + branch[i]
            keep = inside & (at - 3 >= top) & (at - 3 < bottom)
            store_planes(field1, at, jnp.where(keep, value, 0.0), planes)

    def second(g, branch):
        for dy in range(2):
            value = field1[2 * g + dy + 3, 3 : 3 + planes].astype(F32) + branch[dy]
            value = value.astype(BF16).astype(F32)
            normed = normalize([value[:, :, 128 * c : 128 * c + 128] for c in range(depth // 128)])
            chosen = dot(pick_ref[...], normed.reshape(pixels, depth)).astype(BF16)
            half = chosen.shape[0] // 2
            for dx in range(2):
                at = (2 * dy + dx) * depth
                patches[g, :, at : at + depth] = chosen[dx * half : (dx + 1) * half]

    weights = (taps_ref, w_in_ref, w_out_ref, wide, mixed, 256, False)
    run_block(field0, rows + 6, GROUP, 0, *weights, first)
    run_block(field1, rows, 2, 1, *weights, second)
    coarse = dot(patches[...].reshape(-1, 4 * depth), stride_ref[...])
    out_ref[...] = coarse.astype(BF16).reshape(out_ref.shape)


def section_two(
    ends, place_ref, marks_ref, z_ref, spread_ref, pick_ref, taps_ref, w_in_ref, w_out_ref,
    out_ref, field0, field1, wide, mixed,
):
    rows, cols = out_ref.shape[:2]
    width, depth = z_ref.shape[1:]
    planes = width // S
    pixels = planes * S

    def tile_flag(i, j):
        i = jnp.clip((place_ref[0] * rows + i) // TILE2, 0, marks_ref.shape[0] - 1)
        j = jnp.clip((place_ref[1] * cols + j) // TILE2, 0, marks_ref.shape[1] - 1)
        return marks_ref[i, j]

    clear = tile_flag(0, 0) == 1

    @pl.when(jnp.logical_not(clear))
    def _():
        out_ref[...] = z_ref[RING : RING + rows, PAD : PAD + cols, :]

    @pl.when(clear)
    def _():
        columns = column_index(planes)
        top, bottom, inside = picture_edges(place_ref, ends, columns, rows, cols)
        permute_rows(spread_ref, z_ref, field0, 4)

        def first(g, branch):
            for i in range(GROUP):
                at = GROUP * g + i
                own = at - 3
                old = field0[at + 3, 3 : 3 + planes].astype(F32)
                left, mid, right = [tile_flag(own, j) for j in (-1, 0, cols)]
                flag = jnp.where(columns < 0, left, jnp.where(columns < cols, mid, right))
                new = jnp.where(flag == 1, old + branch[i], old)
                keep = inside & (own >= top) & (own < bottom)
                store_planes(field1, at, jnp.where(keep, new, 0.0), planes)

        def second(g, branch):
            for i in range(2):
                at = 2 * g + i
                new = field1[at + 3, 3 : 3 + planes].astype(F32) + branch[i]
                new = new.astype(BF16).reshape(pixels, depth)
                out_ref[at] = dot(pick_ref[...], new).astype(BF16)

        weights = (taps_ref, w_in_ref, w_out_ref, wide, mixed, 512, True)
        run_block(field0, rows + 6, GROUP, 0, *weights, first)
        run_block(field1, rows, 2, 1, *weights, second)


def with_halo(cells):
    axes = ("row", "col")
    counts = [lax.axis_size(axis) for axis in axes]
    even = [lax.axis_index(axis) % 2 == 0 for axis in axes]

    def partner(i, count, outer):
        j = (i - 1 ^ 1) + 1 if outer else i ^ 1
        return j if 0 <= j < count else None

    def edge(array, dim, outer):
        width = (RING, PAD)[dim]
        head = lax.slice_in_dim(array, 0, width, axis=dim)
        tail = lax.slice_in_dim(array, array.shape[dim] - width, array.shape[dim], axis=dim)
        return jnp.where(even[dim], *((head, tail) if outer else (tail, head)))

    def swap(array, moves):
        pairs = []
        for i in range(counts[0]):
            for j in range(counts[1]):
                to = [
                    at if move is None else partner(at, count, move)
                    for at, count, move in zip((i, j), counts, moves)
                ]
                if None not in to:
                    pairs.append((i * counts[1] + j, to[0] * counts[1] + to[1]))
        return lax.ppermute(array, axes, pairs)

    def sides(dim, inner, outer):
        return jnp.where(even[dim], outer, inner), jnp.where(even[dim], inner, outer)

    rows = [edge(cells, 0, outer) for outer in (False, True)]
    above, below = sides(0, *[swap(rows[m], (bool(m), None)) for m in range(2)])
    left, right = sides(1, *[swap(edge(cells, 1, m), (None, m)) for m in (False, True)])
    corners = [
        sides(0, *[swap(edge(rows[m], 1, n), (bool(m), n)) for m in range(2)])
        for n in (False, True)
    ]
    top_left, top_right = sides(1, corners[0][0], corners[1][0])
    bottom_left, bottom_right = sides(1, corners[0][1], corners[1][1])
    bands = [(top_left, above, top_right), (left, cells, right), (bottom_left, below, bottom_right)]
    return jnp.concatenate([jnp.concatenate(band, axis=1) for band in bands], axis=0)


def call(kernel, name, out_shape, scalars, arrays, scratch):
    return pl.pallas_call(
        kernel,
        name=name,
        out_shape=out_shape,
        in_specs=[pl.BlockSpec(memory_space=pltpu.SMEM) for _ in scalars]
        + [pl.BlockSpec(memory_space=pltpu.VMEM) for _ in arrays],
        out_specs=pl.BlockSpec(memory_space=pltpu.VMEM),
        scratch_shapes=[pltpu.VMEM(shape, dtype) for shape, dtype in scratch],
        compiler_params=pltpu.CompilerParams(vmem_limit_bytes=56 * 1024 * 1024),
    )(*scalars, *arrays)


def run_one(ends, place, padded, taps, w_in, w_out, stride):
    rows, width, depth = padded.shape
    rows -= 2 * RING
    planes = width // S
    half = (width - 2 * PAD) // 2
    wide_depth = stride.shape[1]
    columns = [2 * j + dx for dx in range(2) for j in range(half)]
    return call(
        functools.partial(section_one, ends),
        "section_one",
        jax.ShapeDtypeStruct((rows // 2, half, wide_depth), BF16),
        [place],
        [padded, jnp.asarray(spread(width), BF16), jnp.asarray(pick(width, columns), BF16),
         taps, w_in, w_out, stride],
        [
            ((rows + 2 * RING, planes + 6, S, depth), BF16),
            ((rows + 6, planes + 6, S, depth), BF16),
            ((49, 8, depth), F32),
            ((2, depth // 128, GROUP, planes, S, 128), F32),
            ((rows // 2, half, 4 * depth), BF16),
        ],
    )


def run_two(ends, place, marks, padded, taps, w_in, w_out):
    rows, width, depth = padded.shape
    rows -= 2 * RING
    cols = width - 2 * PAD
    planes = width // S
    return call(
        functools.partial(section_two, ends),
        "section_two",
        jax.ShapeDtypeStruct((rows, cols, depth), BF16),
        [place, marks],
        [padded, jnp.asarray(spread(width), BF16), jnp.asarray(pick(width, range(cols)), BF16),
         taps, w_in, w_out],
        [
            ((rows + 2 * RING, planes + 6, S, depth), BF16),
            ((rows + 6, planes + 6, S, depth), BF16),
            ((49, 8, depth), F32),
            ((2, depth // 128, GROUP, planes, S, 128), F32),
        ],
    )


def per_device(
    input_picture,
    spatial_taps_first,
    widening_matrix_first,
    narrowing_matrix_first,
    stride_kernel_matrix,
    spatial_taps_second,
    widening_matrix_second,
    narrowing_matrix_second,
    sky_clarity_marks,
):
    axes = ("row", "col")
    place = jnp.stack([lax.axis_index(axis) for axis in axes]).astype(jnp.int32)
    ends = tuple(lax.axis_size(axis) - 1 for axis in axes)
    coarse = run_one(
        ends,
        place,
        with_halo(input_picture),
        spatial_taps_first,
        widening_matrix_first,
        narrowing_matrix_first,
        stride_kernel_matrix,
    )
    return run_two(
        ends,
        place,
        sky_clarity_marks,
        with_halo(coarse),
        spatial_taps_second,
        widening_matrix_second,
        narrowing_matrix_second,
    )


def solution(mesh):
    placed = (P("row", "col", None), P(), P(), P(), P(), P(), P(), P(), P())
    return jax.shard_map(
        per_device, mesh=mesh, in_specs=placed, out_specs=P("row", "col", None), check_vma=False
    )
```

```python
import functools

import jax
import jax.numpy as jnp
import numpy as np
from jax import lax
from jax.experimental import pallas as pl
from jax.experimental.pallas import tpu as pltpu
from jax.sharding import PartitionSpec as P

TILE2 = 64
EPS = 1e-06
F32 = jnp.float32
BF16 = jnp.bfloat16
S = 16
PAD = 8
RING = 6
GROUP = 2
WIDE_GROUP = 4


def spread(width):
    planes = width // S
    hot = np.zeros((planes + 6, S, width), np.float32)
    for t in range(-3, planes + 3):
        for s in range(S):
            c = planes * s + t
            if 0 <= c < width:
                hot[t + 3, s, c] = 1
    return hot.reshape((planes + 6) * S, width)


def pick(width, columns):
    planes = width // S
    hot = np.zeros((len(columns), width), np.float32)
    for j, c in enumerate(columns):
        s, t = divmod(c + PAD, planes)
        hot[j, t * S + s] = 1
    return hot


def dot(a, b):
    return jnp.dot(a, b, preferred_element_type=F32)


def spread_taps(taps_ref, layer, wide_ref):
    taps = taps_ref[layer].astype(F32)
    for tap in range(49):
        wide_ref[tap] = jnp.broadcast_to(taps[tap : tap + 1], wide_ref.shape[1:])


def depthwise(field_ref, row, wide_ref, planes, lanes):
    total = [None] * planes
    for a in range(7):
        line = field_ref[row + a, :, :, lanes].astype(F32).reshape(planes + 6, S // 8, 8, 128)
        for b in range(7):
            tap = wide_ref[7 * a + b, :, lanes][None]
            for t in range(planes):
                p = line[t + b] * tap
                total[t] = p if total[t] is None else total[t] + p
    return jnp.stack(total).reshape(planes, S, 128)


def normalize(parts):
    depth = 128 * len(parts)
    mean = jnp.sum(functools.reduce(jnp.add, parts), axis=-1, keepdims=True) / depth
    centred = [p - mean for p in parts]
    squares = functools.reduce(jnp.add, [c * c for c in centred])
    variance = jnp.sum(squares, axis=-1, keepdims=True) / depth
    scale = lax.rsqrt(variance + EPS)
    return jnp.concatenate([c * scale for c in centred], axis=-1).astype(BF16)


def twice_gelu(h):
    return (h * (1.0 + lax.erf(h * np.float32(0.5**0.5)))).astype(BF16)


def mlp(flat, w_in_ref, w_out_ref, layer, step):
    hidden = w_in_ref.shape[2]
    total = None
    for c in range(0, hidden, step):
        h = twice_gelu(dot(flat, w_in_ref[layer, :, c : c + step]))
        part = dot(h, w_out_ref[layer, c : c + step, :])
        total = part if total is None else total + part
    return 0.5 * total


def run_block(
    field_ref, count, group, layer, taps_ref, w_in_ref, w_out_ref, wide, mixed, step, ahead, ready, emit
):
    planes, depth = field_ref.shape[1] - 6, field_ref.shape[3]
    chunks = depth // 128
    spread_taps(taps_ref, layer, wide)

    def mix(g):
        for i in range(group):
            for c in range(chunks):
                sums = depthwise(field_ref, group * g + i, wide, planes, pl.ds(128 * c, 128))
                mixed[g % 2, c, i] = sums

    def project(g):
        flat = normalize([mixed[g % 2, c, :group] for c in range(chunks)])
        flat = flat.reshape(group * planes * S, depth)
        branch = mlp(flat, w_in_ref, w_out_ref, layer, step)
        emit(g, branch.reshape(group, planes, S, depth))

    mix(0)
    ready()

    def body(g, carry):
        if ahead:
            mix(g + 1)
        project(g)
        if not ahead:
            mix(g + 1)
        return carry

    last = count // group - 1
    lax.fori_loop(0, last, body, 0)
    project(last)


def store_planes(field_ref, row, values, planes):
    field_ref[row, 3 : 3 + planes] = values.astype(BF16)
    for j in range(3):
        field_ref[row, j] = pltpu.roll(values[planes - 3 + j], 1, 0).astype(BF16)
        field_ref[row, 3 + planes + j] = pltpu.roll(values[j], S - 1, 0).astype(BF16)


def column_index(planes):
    t = lax.broadcasted_iota(jnp.int32, (planes, S, 1), 0)
    s = lax.broadcasted_iota(jnp.int32, (planes, S, 1), 1)
    return planes * s + t - PAD


def permute_rows(hot_refs, source_refs, field_ref):
    spread_ref, middle_ref, sides_ref = hot_refs
    cells_ref, edges_ref, above_ref, below_ref = source_refs
    shape = field_ref.shape[1:]
    rows = cells_ref.shape[0]

    def store(r, values):
        field_ref[r] = values.astype(BF16).reshape(shape)

    def outer(r, carry):
        store(r, dot(spread_ref[...], above_ref[r]))
        store(r + RING + rows, dot(spread_ref[...], below_ref[r]))
        return carry

    def inner(r, carry):
        values = dot(middle_ref[...], cells_ref[r]) + dot(sides_ref[...], edges_ref[r])
        store(r + RING, values)
        return carry

    lax.fori_loop(0, RING, outer, 0, unroll=2)
    lax.fori_loop(0, rows, inner, 0, unroll=4)


def picture_edges(place_ref, ends, columns, rows, cols):
    far = 1 << 20
    top = jnp.where(place_ref[0] == 0, 0, -far)
    bottom = jnp.where(place_ref[0] == ends[0], rows, far)
    left = jnp.where(place_ref[1] == 0, 0, -far)
    right = jnp.where(place_ref[1] == ends[1], cols, far)
    return top, bottom, (columns >= left) & (columns < right)


def section_one(
    ends, place_ref, x_ref, edges_ref, above_ref, below_ref, spread_ref, middle_ref, sides_ref,
    pick_ref, taps_ref, w_in_hbm, w_out_hbm, stride_hbm,
    out_ref, field0, field1, wide, mixed, patches, w_in_ref, w_out_ref, stride_ref, arrived,
):
    rows, depth = x_ref.shape[0], x_ref.shape[2]
    width = spread_ref.shape[1]
    planes = width // S
    pixels = planes * S
    loads = [
        pltpu.make_async_copy(source, target, arrived.at[n])
        for n, (source, target) in enumerate(
            [(w_in_hbm, w_in_ref), (w_out_hbm, w_out_ref), (stride_hbm, stride_ref)]
        )
    ]
    for load in loads:
        load.start()

    def ready():
        for load in loads:
            load.wait()

    columns = column_index(planes)
    top, bottom, inside = picture_edges(place_ref, ends, columns, rows, width - 2 * PAD)
    hot_refs = (spread_ref, middle_ref, sides_ref)
    permute_rows(hot_refs, (x_ref, edges_ref, above_ref, below_ref), field0)

    def first(g, branch):
        for i in range(GROUP):
            at = GROUP * g + i
            value = field0[at + 3, 3 : 3 + planes].astype(F32) + branch[i]
            keep = inside & (at - 3 >= top) & (at - 3 < bottom)
            store_planes(field1, at, jnp.where(keep, value, 0.0), planes)

    def second(g, branch):
        for n in range(WIDE_GROUP):
            dy = n % 2
            value = field1[WIDE_GROUP * g + n + 3, 3 : 3 + planes].astype(F32) + branch[n]
            value = value.astype(BF16).astype(F32)
            normed = normalize([value[:, :, 128 * c : 128 * c + 128] for c in range(depth // 128)])
            chosen = dot(pick_ref[...], normed.reshape(pixels, depth)).astype(BF16)
            half = chosen.shape[0] // 2
            for dx in range(2):
                at = (2 * dy + dx) * depth
                patches[WIDE_GROUP // 2 * g + n // 2, :, at : at + depth] = chosen[dx * half : (dx + 1) * half]

    weights = (taps_ref, w_in_ref, w_out_ref, wide, mixed, 1024, False)
    run_block(field0, rows + 6, GROUP, 0, *weights, ready, first)
    run_block(field1, rows, WIDE_GROUP, 1, *weights, lambda: None, second)
    coarse = dot(patches[...].reshape(-1, 4 * depth), stride_ref[...])
    out_ref[...] = coarse.astype(BF16).reshape(out_ref.shape)


def section_two(
    ends, place_ref, marks_ref, z_ref, edges_ref, above_ref, below_ref, spread_ref, middle_ref,
    sides_ref, pick_ref, taps_ref, w_in_hbm, w_out_hbm,
    out_ref, field0, field1, wide, mixed, w_in_ref, w_out_ref, arrived,
):
    rows, cols, depth = z_ref.shape
    width = spread_ref.shape[1]
    planes = width // S
    pixels = planes * S

    def tile_flag(i, j):
        i = jnp.clip((place_ref[0] * rows + i) // TILE2, 0, marks_ref.shape[0] - 1)
        j = jnp.clip((place_ref[1] * cols + j) // TILE2, 0, marks_ref.shape[1] - 1)
        return marks_ref[i, j]

    clear = tile_flag(0, 0) == 1

    @pl.when(jnp.logical_not(clear))
    def _():
        out_ref[...] = z_ref[...]

    @pl.when(clear)
    def _():
        loads = [
            pltpu.make_async_copy(w_in_hbm, w_in_ref, arrived.at[0]),
            pltpu.make_async_copy(w_out_hbm, w_out_ref, arrived.at[1]),
        ]
        for load in loads:
            load.start()

        def ready():
            for load in loads:
                load.wait()

        columns = column_index(planes)
        top, bottom, inside = picture_edges(place_ref, ends, columns, rows, cols)
        hot_refs = (spread_ref, middle_ref, sides_ref)
        permute_rows(hot_refs, (z_ref, edges_ref, above_ref, below_ref), field0)

        def first(g, branch):
            for i in range(GROUP):
                at = GROUP * g + i
                own = at - 3
                old = field0[at + 3, 3 : 3 + planes].astype(F32)
                left, mid, right = [tile_flag(own, j) for j in (-1, 0, cols)]
                flag = jnp.where(columns < 0, left, jnp.where(columns < cols, mid, right))
                new = jnp.where(flag == 1, old + branch[i], old)
                keep = inside & (own >= top) & (own < bottom)
                store_planes(field1, at, jnp.where(keep, new, 0.0), planes)

        def second(g, branch):
            for i in range(GROUP):
                at = GROUP * g + i
                new = field1[at + 3, 3 : 3 + planes].astype(F32) + branch[i]
                new = new.astype(BF16).reshape(pixels, depth)
                out_ref[at] = dot(pick_ref[...], new).astype(BF16)

        weights = (taps_ref, w_in_ref, w_out_ref, wide, mixed, 1024, True)
        run_block(field0, rows + 6, GROUP, 0, *weights, ready, first)
        run_block(field1, rows, GROUP, 1, *weights, lambda: None, second)


def halo(cells):
    def swap(axis, head, tail):
        count = lax.axis_size(axis)
        even = lax.axis_index(axis) % 2 == 0
        inner = [(i, i ^ 1) for i in range(count)]
        outer = [(i, (i - 1 ^ 1) + 1) for i in range(1, count - 1)]
        near = lax.ppermute(jnp.where(even, tail, head), axis, inner)
        far = lax.ppermute(jnp.where(even, head, tail), axis, outer)
        return jnp.where(even, far, near), jnp.where(even, near, far)

    left, right = swap("col", cells[:, :PAD], cells[:, -PAD:])

    def band(rows):
        return jnp.concatenate([left[rows], cells[rows], right[rows]], axis=1)

    above, below = swap("row", band(slice(0, RING)), band(slice(-RING, None)))
    return [cells, jnp.concatenate([left, right], axis=1), above, below]


def call(kernel, name, out_shape, scalars, arrays, weights, scratch):
    spaces = [pltpu.SMEM] * len(scalars) + [pltpu.VMEM] * len(arrays) + [pl.ANY] * len(weights)
    buffers = scratch + [(w.shape, w.dtype) for w in weights]
    return pl.pallas_call(
        kernel,
        name=name,
        out_shape=out_shape,
        in_specs=[pl.BlockSpec(memory_space=space) for space in spaces],
        out_specs=pl.BlockSpec(memory_space=pltpu.VMEM),
        scratch_shapes=[pltpu.VMEM(shape, dtype) for shape, dtype in buffers]
        + [pltpu.SemaphoreType.DMA((len(weights),))],
        compiler_params=pltpu.CompilerParams(vmem_limit_bytes=56 * 1024 * 1024),
    )(*scalars, *arrays, *weights)


def one_hots(width, columns):
    hot = spread(width)
    sides = np.concatenate([hot[:, :PAD], hot[:, -PAD:]], axis=1)
    return [jnp.asarray(m, BF16) for m in (hot, hot[:, PAD:-PAD], sides, pick(width, columns))]


def run_one(ends, place, sources, taps, w_in, w_out, stride):
    rows, cols, depth = sources[0].shape
    width = cols + 2 * PAD
    planes = width // S
    columns = [2 * j + dx for dx in range(2) for j in range(cols // 2)]
    return call(
        functools.partial(section_one, ends),
        "section_one",
        jax.ShapeDtypeStruct((rows // 2, cols // 2, stride.shape[1]), BF16),
        [place],
        [*sources, *one_hots(width, columns), taps],
        [w_in, w_out, stride],
        [
            ((rows + 2 * RING, planes + 6, S, depth), BF16),
            ((rows + 6, planes + 6, S, depth), BF16),
            ((49, 8, depth), F32),
            ((2, depth // 128, WIDE_GROUP, planes, S, 128), F32),
            ((rows // 2, cols // 2, 4 * depth), BF16),
        ],
    )


def run_two(ends, place, marks, sources, taps, w_in, w_out):
    rows, cols, depth = sources[0].shape
    width = cols + 2 * PAD
    planes = width // S
    return call(
        functools.partial(section_two, ends),
        "section_two",
        jax.ShapeDtypeStruct((rows, cols, depth), BF16),
        [place, marks],
        [*sources, *one_hots(width, range(cols)), taps],
        [w_in, w_out],
        [
            ((rows + 2 * RING, planes + 6, S, depth), BF16),
            ((rows + 6, planes + 6, S, depth), BF16),
            ((49, 8, depth), F32),
            ((2, depth // 128, GROUP, planes, S, 128), F32),
        ],
    )


def per_device(
    input_picture,
    spatial_taps_first,
    widening_matrix_first,
    narrowing_matrix_first,
    stride_kernel_matrix,
    spatial_taps_second,
    widening_matrix_second,
    narrowing_matrix_second,
    sky_clarity_marks,
):
    axes = ("row", "col")
    place = jnp.stack([lax.axis_index(axis) for axis in axes]).astype(jnp.int32)
    ends = tuple(lax.axis_size(axis) - 1 for axis in axes)
    coarse = run_one(
        ends,
        place,
        halo(input_picture),
        spatial_taps_first,
        widening_matrix_first,
        narrowing_matrix_first,
        stride_kernel_matrix,
    )
    return run_two(
        ends,
        place,
        sky_clarity_marks,
        halo(coarse),
        spatial_taps_second,
        widening_matrix_second,
        narrowing_matrix_second,
    )


def solution(mesh):
    placed = (P("row", "col", None), P(), P(), P(), P(), P(), P(), P(), P())
    return jax.shard_map(
        per_device, mesh=mesh, in_specs=placed, out_specs=P("row", "col", None), check_vma=False
    )
```

```python
import functools

import jax
import jax.numpy as jnp
import numpy as np
from jax import lax
from jax.experimental import pallas as pl
from jax.experimental.pallas import tpu as pltpu
from jax.sharding import PartitionSpec as P

TILE2 = 64
EPS = 1e-06
F32 = jnp.float32
BF16 = jnp.bfloat16
S = 16
PAD = 8
RING = 6
GROUP = 2
WIDE_GROUP = 4


def spread(width):
    planes = width // S
    hot = np.zeros((planes + 6, S, width), np.float32)
    for t in range(-3, planes + 3):
        for s in range(S):
            c = planes * s + t
            if 0 <= c < width:
                hot[t + 3, s, c] = 1
    return hot.reshape((planes + 6) * S, width)


def pick(width, columns):
    planes = width // S
    hot = np.zeros((len(columns), width), np.float32)
    for j, c in enumerate(columns):
        s, t = divmod(c + PAD, planes)
        hot[j, t * S + s] = 1
    return hot


def dot(a, b):
    return jnp.dot(a, b, preferred_element_type=F32)


def spread_taps(taps_ref, layer, wide_ref):
    taps = taps_ref[layer].astype(F32)
    for tap in range(49):
        wide_ref[tap] = jnp.broadcast_to(taps[tap : tap + 1], wide_ref.shape[1:])


def depthwise(field_ref, row, wide_ref, planes, lanes):
    total = [None] * planes
    for a in range(7):
        line = field_ref[row + a, :, :, lanes].astype(F32).reshape(planes + 6, S // 8, 8, 128)
        for b in range(7):
            tap = wide_ref[7 * a + b, :, lanes][None]
            for t in range(planes):
                p = line[t + b] * tap
                total[t] = p if total[t] is None else total[t] + p
    return jnp.stack(total).reshape(planes, S, 128)


def normalize(parts):
    depth = 128 * len(parts)
    mean = jnp.sum(functools.reduce(jnp.add, parts), axis=-1, keepdims=True) / depth
    centred = [p - mean for p in parts]
    squares = functools.reduce(jnp.add, [c * c for c in centred])
    variance = jnp.sum(squares, axis=-1, keepdims=True) / depth
    scale = lax.rsqrt(variance + EPS)
    return jnp.concatenate([c * scale for c in centred], axis=-1).astype(BF16)


def twice_gelu(h):
    return (h * (1.0 + lax.erf(h * np.float32(0.5**0.5)))).astype(BF16)


def mlp(flat, w_in_ref, w_out_ref, layer, step):
    hidden = w_in_ref.shape[2]
    total = None
    for c in range(0, hidden, step):
        h = twice_gelu(dot(flat, w_in_ref[layer, :, c : c + step]))
        part = dot(h, w_out_ref[layer, c : c + step, :])
        total = part if total is None else total + part
    return 0.5 * total


def run_block(
    field_ref, count, group, layer, taps_ref, w_in_ref, w_out_ref, wide, mixed, step, ahead, ready, emit
):
    planes, depth = field_ref.shape[1] - 6, field_ref.shape[3]
    chunks = depth // 128
    spread_taps(taps_ref, layer, wide)

    def mix(g):
        for i in range(group):
            for c in range(chunks):
                sums = depthwise(field_ref, group * g + i, wide, planes, pl.ds(128 * c, 128))
                mixed[g % 2, c, i] = sums

    def project(g):
        flat = normalize([mixed[g % 2, c, :group] for c in range(chunks)])
        flat = flat.reshape(group * planes * S, depth)
        branch = mlp(flat, w_in_ref, w_out_ref, layer, step)
        emit(g, branch.reshape(group, planes, S, depth))

    mix(0)
    ready()

    def body(g, carry):
        if ahead:
            mix(g + 1)
        project(g)
        if not ahead:
            mix(g + 1)
        return carry

    last = count // group - 1
    lax.fori_loop(0, last, body, 0)
    project(last)


def store_planes(field_ref, row, values, planes):
    field_ref[row, 3 : 3 + planes] = values.astype(BF16)
    for j in range(3):
        field_ref[row, j] = pltpu.roll(values[planes - 3 + j], 1, 0).astype(BF16)
        field_ref[row, 3 + planes + j] = pltpu.roll(values[j], S - 1, 0).astype(BF16)


def column_index(planes):
    t = lax.broadcasted_iota(jnp.int32, (planes, S, 1), 0)
    s = lax.broadcasted_iota(jnp.int32, (planes, S, 1), 1)
    return planes * s + t - PAD


def permute_rows(place_ref, hot_refs, source_refs, field_ref):
    spread_ref, middle_ref, sides_ref = hot_refs
    cells_ref, edges_ref, near_ref, far_ref = source_refs
    shape = field_ref.shape[1:]
    rows = cells_ref.shape[0]
    odd = place_ref[0] % 2
    below = RING + rows

    def store(r, values):
        field_ref[r] = values.astype(BF16).reshape(shape)

    def outer(r, carry):
        store(r + below * (1 - odd), dot(spread_ref[...], near_ref[r]))
        store(r + below * odd, dot(spread_ref[...], far_ref[r]))
        return carry

    def inner(r, carry):
        values = dot(middle_ref[...], cells_ref[r]) + dot(sides_ref[...], edges_ref[r])
        store(r + RING, values)
        return carry

    lax.fori_loop(0, RING, outer, 0, unroll=2)
    lax.fori_loop(0, rows, inner, 0, unroll=4)


def picture_edges(place_ref, ends, columns, rows, cols):
    far = 1 << 20
    top = jnp.where(place_ref[0] == 0, 0, -far)
    bottom = jnp.where(place_ref[0] == ends[0], rows, far)
    left = jnp.where(place_ref[1] == 0, 0, -far)
    right = jnp.where(place_ref[1] == ends[1], cols, far)
    return top, bottom, (columns >= left) & (columns < right)


def section_one(
    ends, place_ref, x_ref, edges_ref, near_ref, far_ref, spread_ref, middle_ref, sides_ref,
    pick_ref, taps_ref, w_in_hbm, w_out_hbm, stride_hbm,
    out_ref, field0, field1, wide, mixed, patches, w_in_ref, w_out_ref, stride_ref, arrived,
):
    rows, depth = x_ref.shape[0], x_ref.shape[2]
    width = spread_ref.shape[1]
    planes = width // S
    pixels = planes * S
    loads = [
        pltpu.make_async_copy(source, target, arrived.at[n])
        for n, (source, target) in enumerate(
            [(w_in_hbm, w_in_ref), (w_out_hbm, w_out_ref), (stride_hbm, stride_ref)]
        )
    ]
    for load in loads:
        load.start()

    def ready():
        for load in loads:
            load.wait()

    columns = column_index(planes)
    top, bottom, inside = picture_edges(place_ref, ends, columns, rows, width - 2 * PAD)
    hot_refs = (spread_ref, middle_ref, sides_ref)
    permute_rows(place_ref, hot_refs, (x_ref, edges_ref, near_ref, far_ref), field0)

    def first(g, branch):
        for i in range(GROUP):
            at = GROUP * g + i
            value = field0[at + 3, 3 : 3 + planes].astype(F32) + branch[i]
            keep = inside & (at - 3 >= top) & (at - 3 < bottom)
            store_planes(field1, at, jnp.where(keep, value, 0.0), planes)

    def second(g, branch):
        for n in range(WIDE_GROUP):
            dy = n % 2
            value = field1[WIDE_GROUP * g + n + 3, 3 : 3 + planes].astype(F32) + branch[n]
            value = value.astype(BF16).astype(F32)
            normed = normalize([value[:, :, 128 * c : 128 * c + 128] for c in range(depth // 128)])
            chosen = dot(pick_ref[...], normed.reshape(pixels, depth)).astype(BF16)
            half = chosen.shape[0] // 2
            for dx in range(2):
                at = (2 * dy + dx) * depth
                patches[WIDE_GROUP // 2 * g + n // 2, :, at : at + depth] = chosen[dx * half : (dx + 1) * half]

    weights = (taps_ref, w_in_ref, w_out_ref, wide, mixed, 1024, False)
    run_block(field0, rows + 6, GROUP, 0, *weights, ready, first)
    run_block(field1, rows, WIDE_GROUP, 1, *weights, lambda: None, second)
    coarse = dot(patches[...].reshape(-1, 4 * depth), stride_ref[...])
    out_ref[...] = coarse.astype(BF16).reshape(out_ref.shape)


def section_two(
    ends, place_ref, marks_ref, z_ref, edges_ref, near_ref, far_ref, spread_ref, middle_ref,
    sides_ref, pick_ref, taps_ref, w_in_hbm, w_out_hbm,
    out_ref, field0, field1, wide, mixed, w_in_ref, w_out_ref, arrived,
):
    rows, cols, depth = z_ref.shape
    width = spread_ref.shape[1]
    planes = width // S
    pixels = planes * S

    def tile_flag(i, j):
        i = jnp.clip((place_ref[0] * rows + i) // TILE2, 0, marks_ref.shape[0] - 1)
        j = jnp.clip((place_ref[1] * cols + j) // TILE2, 0, marks_ref.shape[1] - 1)
        return marks_ref[i, j]

    clear = tile_flag(0, 0) == 1

    @pl.when(jnp.logical_not(clear))
    def _():
        out_ref[...] = z_ref[...]

    @pl.when(clear)
    def _():
        loads = [
            pltpu.make_async_copy(w_in_hbm, w_in_ref, arrived.at[0]),
            pltpu.make_async_copy(w_out_hbm, w_out_ref, arrived.at[1]),
        ]
        for load in loads:
            load.start()

        def ready():
            for load in loads:
                load.wait()

        columns = column_index(planes)
        top, bottom, inside = picture_edges(place_ref, ends, columns, rows, cols)
        hot_refs = (spread_ref, middle_ref, sides_ref)
        permute_rows(place_ref, hot_refs, (z_ref, edges_ref, near_ref, far_ref), field0)

        def first(g, branch):
            for i in range(GROUP):
                at = GROUP * g + i
                own = at - 3
                old = field0[at + 3, 3 : 3 + planes].astype(F32)
                left, mid, right = [tile_flag(own, j) for j in (-1, 0, cols)]
                flag = jnp.where(columns < 0, left, jnp.where(columns < cols, mid, right))
                new = jnp.where(flag == 1, old + branch[i], old)
                keep = inside & (own >= top) & (own < bottom)
                store_planes(field1, at, jnp.where(keep, new, 0.0), planes)

        def second(g, branch):
            for i in range(GROUP):
                at = GROUP * g + i
                new = field1[at + 3, 3 : 3 + planes].astype(F32) + branch[i]
                new = new.astype(BF16).reshape(pixels, depth)
                out_ref[at] = dot(pick_ref[...], new).astype(BF16)

        weights = (taps_ref, w_in_ref, w_out_ref, wide, mixed, 1024, True)
        run_block(field0, rows + 6, GROUP, 0, *weights, ready, first)
        run_block(field1, rows, GROUP, 1, *weights, lambda: None, second)


def halo(cells):
    def swap(axis, head, tail):
        count = lax.axis_size(axis)
        even = lax.axis_index(axis) % 2 == 0
        inner = [(i, i ^ 1) for i in range(count)]
        outer = [(i, (i - 1 ^ 1) + 1) for i in range(1, count - 1)]
        near = lax.ppermute(jnp.where(even, tail, head), axis, inner)
        far = lax.ppermute(jnp.where(even, head, tail), axis, outer)
        return even, near, far

    even, near, far = swap("col", cells[:, :PAD], cells[:, -PAD:])
    left, right = jnp.where(even, far, near), jnp.where(even, near, far)

    def band(rows):
        return jnp.concatenate([left[rows], cells[rows], right[rows]], axis=1)

    _, near, far = swap("row", band(slice(0, RING)), band(slice(-RING, None)))
    return [cells, jnp.concatenate([left, right], axis=1), near, far]


def call(kernel, name, out_shape, scalars, arrays, weights, scratch):
    spaces = [pltpu.SMEM] * len(scalars) + [pltpu.VMEM] * len(arrays) + [pl.ANY] * len(weights)
    buffers = scratch + [(w.shape, w.dtype) for w in weights]
    return pl.pallas_call(
        kernel,
        name=name,
        out_shape=out_shape,
        in_specs=[pl.BlockSpec(memory_space=space) for space in spaces],
        out_specs=pl.BlockSpec(memory_space=pltpu.VMEM),
        scratch_shapes=[pltpu.VMEM(shape, dtype) for shape, dtype in buffers]
        + [pltpu.SemaphoreType.DMA((len(weights),))],
        compiler_params=pltpu.CompilerParams(vmem_limit_bytes=56 * 1024 * 1024),
    )(*scalars, *arrays, *weights)


def one_hots(width, columns):
    hot = spread(width)
    sides = np.concatenate([hot[:, :PAD], hot[:, -PAD:]], axis=1)
    return [jnp.asarray(m, BF16) for m in (hot, hot[:, PAD:-PAD], sides, pick(width, columns))]


def run_one(ends, place, sources, taps, w_in, w_out, stride):
    rows, cols, depth = sources[0].shape
    width = cols + 2 * PAD
    planes = width // S
    columns = [2 * j + dx for dx in range(2) for j in range(cols // 2)]
    return call(
        functools.partial(section_one, ends),
        "section_one",
        jax.ShapeDtypeStruct((rows // 2, cols // 2, stride.shape[1]), BF16),
        [place],
        [*sources, *one_hots(width, columns), taps],
        [w_in, w_out, stride],
        [
            ((rows + 2 * RING, planes + 6, S, depth), BF16),
            ((rows + 6, planes + 6, S, depth), BF16),
            ((49, 8, depth), F32),
            ((2, depth // 128, WIDE_GROUP, planes, S, 128), F32),
            ((rows // 2, cols // 2, 4 * depth), BF16),
        ],
    )


def run_two(ends, place, marks, sources, taps, w_in, w_out):
    rows, cols, depth = sources[0].shape
    width = cols + 2 * PAD
    planes = width // S
    return call(
        functools.partial(section_two, ends),
        "section_two",
        jax.ShapeDtypeStruct((rows, cols, depth), BF16),
        [place, marks],
        [*sources, *one_hots(width, range(cols)), taps],
        [w_in, w_out],
        [
            ((rows + 2 * RING, planes + 6, S, depth), BF16),
            ((rows + 6, planes + 6, S, depth), BF16),
            ((49, 8, depth), F32),
            ((2, depth // 128, GROUP, planes, S, 128), F32),
        ],
    )


def per_device(
    input_picture,
    spatial_taps_first,
    widening_matrix_first,
    narrowing_matrix_first,
    stride_kernel_matrix,
    spatial_taps_second,
    widening_matrix_second,
    narrowing_matrix_second,
    sky_clarity_marks,
):
    axes = ("row", "col")
    place = jnp.stack([lax.axis_index(axis) for axis in axes]).astype(jnp.int32)
    ends = tuple(lax.axis_size(axis) - 1 for axis in axes)
    coarse = run_one(
        ends,
        place,
        halo(input_picture),
        spatial_taps_first,
        widening_matrix_first,
        narrowing_matrix_first,
        stride_kernel_matrix,
    )
    return run_two(
        ends,
        place,
        sky_clarity_marks,
        halo(coarse),
        spatial_taps_second,
        widening_matrix_second,
        narrowing_matrix_second,
    )


def solution(mesh):
    placed = (P("row", "col", None), P(), P(), P(), P(), P(), P(), P(), P())
    return jax.shard_map(
        per_device, mesh=mesh, in_specs=placed, out_specs=P("row", "col", None), check_vma=False
    )
```
